32 devices in a mesh: groups: 2 (over y), seq: 4 (over z), mp: 2 (over x), enc: 2 (over core).
Axes of the slice: x: 2, y: 2, z: 4, core: 2. Of those that a mesh axis runs over, the one named last changes fastest.
Arguments:
- tokens: bfloat16 [4096, 4096], P(('groups', 'seq'), ('mp', 'enc')), parts along dimension 0, may hold values from -6 to 6
- nbr_feats: bfloat16 [192, 128, 4096], P(('groups', 'seq'), None, ('mp', 'enc')), parts along dimension 0, may hold values from -6 to 6
- counts: int32 [8], P('groups'), parts along dimension 0, may hold values from 8 to 24, as said below
- slot_target: int32 [192], P(('groups', 'seq')), parts along dimension 0, may hold values from 0 to 63, as said below
- w_query: bfloat16 [4096, 512], P(None, ('mp', 'enc')), may hold values from -32 to 32
- w_keyval: bfloat16 [4096, 512], P(None, ('mp', 'enc')), may hold values from -1 to 1
Outputs:
- attended: bfloat16 [4096, 512], P(('groups', 'seq'), ('mp', 'enc')), parts along dimension 0
The draws below stay inside these ranges and needn't reach their ends.
There are 2 independent parts, one for each index of `groups`. The reference program is written for one: setup_inputs(seed, part) draws one part's arguments, and reference() takes and returns one part's arrays. A program takes and returns all parts, laid end to end along the dimension named above; an argument that names none is the same for every part. Nothing has to cross between parts.
Inputs may be any that keep to these rules, and one draw needn't show every extreme that they name: Each seq index's live slots are its first counts slots; the counts sum to 64. `slot_target`: A live slot holds neighbour o * 16 + l of the spans of seq index o; every neighbour is held by exactly one live slot; the live slots of one seq index hold at most 8 neighbours of any one seq index; dead slots hold arbitrary values of the range.
All inputs are finite; a program needn't handle non-finite values.
Results may differ from the reference program's by a relative error of at most 0.003.
The reference program's roundings to bfloat16 on the way count: a program that leaves them out, or rounds other values in their place, can miss the bound.
Values may be sent and summed in bfloat16 or wider, within the bound.
A program may use at most 128 MiB of HBM per device.

```python
import math
import jax
import jax.numpy as jnp
from jax import lax

D = 4096
HD = 128
SPAN = 64
NBR = 2
RLEN = 128
KV_HEADS = 2
Q_HEADS = 4
NB_SEQ = 16
ENC_CAP = 24
TOKENS = 2048
NB_ALL = 64
SLOTS = 96
N_SEQ = 4


def shuffled_positions(sub_key):
    return jax.random.permutation(sub_key, NB_SEQ)


def routing_tables(key):
    base_key = jax.random.fold_in(key, 17)
    keys_list = jax.random.split(base_key, 7)
    half_share = NB_SEQ // 2
    pair_cap = max(2, 2 * NB_SEQ // N_SEQ)
    rank_order = jax.random.permutation(keys_list[0], N_SEQ)
    shifts = jax.random.randint(keys_list[1], (N_SEQ // 2,), 0, half_share + 1)
    forced = jax.random.randint(keys_list[2], (), 0, N_SEQ // 2)
    shifts = jnp.where(jnp.arange(N_SEQ // 2) == forced, half_share, shifts)
    paired = jnp.stack([NB_SEQ + shifts, NB_SEQ - shifts], axis=1).reshape(N_SEQ)
    counts = jnp.zeros((N_SEQ,), jnp.int32).at[rank_order].set(paired.astype(jnp.int32))
    starts = jnp.cumsum(counts) - counts
    owner_order = jax.random.permutation(keys_list[3], N_SEQ)
    local_keys = jax.random.split(keys_list[4], N_SEQ)
    local_order = jax.vmap(shuffled_positions)(local_keys)
    places = jnp.arange(NB_SEQ * N_SEQ)
    owners = owner_order[places // pair_cap % N_SEQ]
    occurrence = places // (pair_cap * N_SEQ) * pair_cap + places % pair_cap
    targets = owners * NB_SEQ + local_order[owners, occurrence]
    slot_ids = jnp.arange(ENC_CAP)
    live_slots = slot_ids[None, :] < counts[:, None]
    noise_draw = jax.random.randint(keys_list[5], (N_SEQ, ENC_CAP), 0, 1 << 20)
    scores = jnp.where(live_slots, noise_draw * ENC_CAP + slot_ids[None, :], (1 << 26) + slot_ids[None, :])
    slot_order = jnp.argsort(scores, axis=1)
    picked = jnp.clip(starts[:, None] + slot_order, 0, NB_SEQ * N_SEQ - 1)
    filler = jax.random.randint(keys_list[6], (N_SEQ, ENC_CAP), 0, NB_SEQ * N_SEQ)
    slot_target = jnp.where(live_slots, targets[picked], filler)
    return (counts, slot_target.reshape(N_SEQ * ENC_CAP).astype(jnp.int32))


def draw_counts(key, part):
    return routing_tables(key)[0]


def draw_slot_target(key, part):
    return routing_tables(key)[1]


def weight_base(key):
    return jax.random.normal(jax.random.fold_in(key, 101), (D, KV_HEADS, HD), jnp.float32)


def draw_w_keyval(key, part):
    base = weight_base(key)
    others = jax.random.normal(jax.random.fold_in(key, 202), (D, KV_HEADS, HD), jnp.float32)
    stacked = jnp.stack([base, others], axis=2) / math.sqrt(D)
    stacked = jnp.clip(stacked, -1.0, 1.0)
    return stacked.reshape(D, KV_HEADS * 2 * HD).astype(jnp.bfloat16)


def draw_w_query(key, part):
    noise_draw = jax.random.normal(jax.random.fold_in(key, 303), (D, KV_HEADS, 2, HD), jnp.float32)
    mixed = noise_draw
    scaled = jnp.clip(mixed / math.sqrt(D), -32.0, 32.0)
    return scaled.reshape(D, KV_HEADS * 2 * HD).astype(jnp.bfloat16)


def block_scale(rng, dims, shards, least, high):
    def one(axis_at, shards_of):
        steps = jax.random.uniform(jax.random.fold_in(jax.random.fold_in(rng, 6), axis_at), (shards_of,), jnp.float32, least / len(shards), high / len(shards))
        return jnp.repeat(jnp.exp(steps), dims[axis_at] // shards_of).reshape((-1,) + (1,) * (len(dims) - axis_at - 1))

    level = one(*shards[0])
    for cut in shards[1:]:
        level = level * one(*cut)
    return level


def scatter_about(own_key, shape, width, limit, shards=(), kind=jnp.bfloat16):
    values = jax.random.normal(own_key, shape, jnp.float32) * width
    if len(shards) > 0:
        values = block_scale(own_key, shape, shards, -0.22, 0.18) * values
    return jnp.clip(values, min=-limit, max=limit).astype(kind)


def setup_inputs(seed: int = 0, part: int = 0) -> dict:
    arg_keys = jax.random.split(jax.random.key(seed), 7)
    own_keys = jax.random.split(jax.random.fold_in(arg_keys[6], part), 7)
    tokens = scatter_about(own_keys[0], (TOKENS, D), 1.0, 6.0, ((0, 4), (1, 4)))
    nbr_feats = scatter_about(own_keys[1], (SLOTS, RLEN, D), 1.0, 6.0, ((0, 4), (2, 4)))
    counts = draw_counts(jax.random.fold_in(jax.random.fold_in(arg_keys[6], part), 71), part)
    slot_target = draw_slot_target(jax.random.fold_in(jax.random.fold_in(arg_keys[6], part), 71), part)
    w_query = draw_w_query(jax.random.fold_in(arg_keys[6], 71), part)
    w_keyval = draw_w_keyval(jax.random.fold_in(arg_keys[6], 71), part)
    return {"tokens": tokens, "nbr_feats": nbr_feats, "counts": counts, "slot_target": slot_target, "w_query": w_query, "w_keyval": w_keyval}


epsilon = 1e-05

def settle(value):
    return lax.optimization_barrier(value.astype(jnp.bfloat16)).astype(jnp.float32)

def reference(tokens, nbr_feats, counts, slot_target, w_query, w_keyval):
    slot_ids = jnp.arange(SLOTS, dtype=jnp.int32)
    slot_owner = (slot_ids // ENC_CAP).astype(jnp.int32)
    live_slots = slot_ids % ENC_CAP < counts[slot_owner]
    where_to = jnp.where(live_slots, slot_target, NB_ALL).astype(jnp.int32)
    source = jnp.zeros((NB_ALL,), jnp.int32).at[where_to].set(slot_ids, mode='drop')

    def encode_one(slot):
        features = lax.dynamic_index_in_dim(nbr_feats, slot, 0, keepdims=False)
        product = jnp.dot(features, w_keyval, preferred_element_type=jnp.float32)
        widened = features.astype(jnp.float32)
        scale_rows = lax.rsqrt(lax.optimization_barrier(jnp.sum(widened * widened, axis=1)) / D + epsilon)
        return (product * scale_rows[:, None]).astype(jnp.bfloat16)
    encoded = lax.map(encode_one, source)
    product = jnp.dot(tokens, w_query, preferred_element_type=jnp.float32)
    widened = tokens.astype(jnp.float32)
    scale_rows = lax.rsqrt(lax.optimization_barrier(jnp.sum(widened * widened, axis=1)) / D + epsilon) * HD ** (-0.5)
    query = settle(product * scale_rows[:, None])
    spans = TOKENS // SPAN
    query = query.reshape(spans, SPAN, KV_HEADS, 2, HD)
    pairs = encoded.reshape(spans, NBR, RLEN, KV_HEADS, 2, HD)
    key_rows = pairs[:, :, :, :, 0, :].reshape(spans, NBR * RLEN, KV_HEADS, HD)
    value_rows = pairs[:, :, :, :, 1, :].reshape(spans, NBR * RLEN, KV_HEADS, HD)
    zero_block = jnp.zeros((1, NBR * RLEN, KV_HEADS, HD), jnp.bfloat16)
    context_keys = jnp.concatenate([zero_block, key_rows[:-1]], axis=0).astype(jnp.float32)
    context_values = jnp.concatenate([zero_block, value_rows[:-1]], axis=0).astype(jnp.float32)
    scores = jnp.einsum('cqhgd,ckhd->cqhgk', query, context_keys)
    weights = settle(jax.nn.softmax(scores, axis=-1))
    attended = jnp.einsum('cqhgk,ckhd->cqhgd', weights, context_values)
    return attended.astype(jnp.bfloat16).reshape(TOKENS, Q_HEADS * HD)
```

```python
import jax
import jax.numpy as jnp
from jax import lax
from jax.sharding import PartitionSpec as P

D = 4096
SPAN = 64
NBR = 2
RLEN = 128
CH_SEQ = 8
NB_SEQ = 16
ENC_CAP = 24


epsilon = 1e-05


def partner_2(block, axis, stride):
    count = lax.axis_size(axis)
    route = []
    for low in range(count):
        high = low | 1 << stride
        if high != low and high < count:
            route += [(low, high), (high, low)]
    return lax.ppermute(block, axis, route)


def passed_along(block, axis, distance):
    devices = range(lax.axis_size(axis))
    route = [(i - distance, i) for i in devices if i - distance in devices]
    return lax.ppermute(block, axis, route)


def project_fold(weight, piece):
    width = piece.shape[-1]
    flat_rows = piece.reshape(-1, width)
    mine = lax.all_to_all(weight, ("mp", "enc"), split_axis=0, concat_axis=1, tiled=True)
    partial = jnp.dot(flat_rows, mine, preferred_element_type=jnp.float32)
    running = lax.psum_scatter(partial, ("mp", "enc"), scatter_dimension=1, tiled=True)
    widened = flat_rows.astype(jnp.float32)
    squares = lax.psum(jnp.sum(widened * widened, axis=1), ("mp", "enc"))
    return (running, squares)


def normalized(carry, factor):
    running, squares = carry
    scale_rows = lax.rsqrt(squares / D + epsilon) * factor
    return (running * scale_rows[:, None]).astype(jnp.bfloat16)


def routing_plan(slot_target, counts, pair_cap):
    seq_count = counts.shape[0]
    seq_here = lax.axis_index("seq")
    live_count = jnp.sum(jnp.where(jnp.arange(seq_count) == seq_here, counts, 0))
    slot_ids = jnp.arange(ENC_CAP)
    live_slots = slot_ids < live_count
    owner_of = slot_target // NB_SEQ
    position = slot_target % NB_SEQ
    same_owner = (
        (owner_of[:, None] == owner_of[None, :])
        & live_slots[None, :]
        & (slot_ids[None, :] < slot_ids[:, None])
    )
    rank_within = jnp.sum(same_owner.astype(jnp.int32), axis=1)
    target_slot = owner_of * pair_cap + rank_within
    buffer_ids = jnp.arange(seq_count * pair_cap)
    chosen = (buffer_ids[:, None] == target_slot[None, :]) & live_slots[None, :]
    sent_ids = jnp.sum(jnp.where(chosen, position[None, :] + 1, 0), axis=1) - 1
    return (chosen, sent_ids.reshape(seq_count, pair_cap))


def pack_rows(chosen, payload, seq_count, pair_cap):
    packed = jnp.dot(chosen.astype(jnp.bfloat16), payload, preferred_element_type=jnp.float32)
    return packed.astype(jnp.bfloat16).reshape(seq_count, pair_cap, payload.shape[1])


def place_rows(received, received_ids):
    flat_rows = received.reshape(-1, received.shape[-1])
    picker = received_ids.reshape(1, -1) == jnp.arange(NB_SEQ)[:, None]
    placed = jnp.dot(picker.astype(jnp.bfloat16), flat_rows, preferred_element_type=jnp.float32)
    return placed.astype(jnp.bfloat16)


def local(tokens, nbr_feats, counts, slot_target, w_query, w_keyval):
    seq_count = lax.axis_size("seq")
    pair_cap = max(2, 2 * NB_SEQ // seq_count)
    head_size = w_keyval.shape[1]
    chosen, sent_ids = routing_plan(slot_target, counts, pair_cap)
    folded = project_fold(w_keyval, nbr_feats)
    encoded = normalized(folded, 1.0).reshape(ENC_CAP, RLEN * head_size)
    packed = pack_rows(chosen, encoded, seq_count, pair_cap)
    received, received_ids = (
        lax.all_to_all(packed, "seq", split_axis=0, concat_axis=0, tiled=True),
        lax.all_to_all(sent_ids, "seq", split_axis=0, concat_axis=0, tiled=True),
    )
    own_half = place_rows(received, received_ids).reshape(NB_SEQ, RLEN, head_size)
    partner = partner_2(own_half, "enc", 0)
    first_lane = lax.axis_index("enc") == 0
    key_rows = jnp.where(first_lane, own_half, partner).reshape(CH_SEQ, NBR * RLEN, head_size)
    value_rows = jnp.where(first_lane, partner, own_half).reshape(CH_SEQ, NBR * RLEN, head_size)
    prior_keys, prior_values = passed_along((key_rows[-1], value_rows[-1]), "seq", 1)
    context_keys = jnp.concatenate([prior_keys[None], key_rows[:-1]], axis=0)
    context_values = jnp.concatenate([prior_values[None], value_rows[:-1]], axis=0)
    folded_tokens = project_fold(w_query, tokens)
    queries = normalized(folded_tokens, head_size ** (-0.5)).reshape(CH_SEQ, SPAN, head_size)
    scores = jnp.einsum("cqd,ckd->cqk", queries, context_keys, preferred_element_type=jnp.float32)
    weights = jax.nn.softmax(scores, axis=-1).astype(jnp.bfloat16)
    attended = jnp.einsum(
        "cqk,ckd->cqd", weights, context_values, preferred_element_type=jnp.float32
    )
    return attended.astype(jnp.bfloat16).reshape(CH_SEQ * SPAN, head_size)


def solution(mesh):
    placed = (
        P(("groups", "seq"), ("mp", "enc")),
        P(("groups", "seq"), None, ("mp", "enc")),
        P("groups"),
        P(("groups", "seq")),
        P(None, ("mp", "enc")),
        P(None, ("mp", "enc")),
    )
    return jax.shard_map(
        local,
        mesh=mesh,
        in_specs=placed,
        out_specs=P(("groups", "seq"), ("mp", "enc")),
        check_vma=False,
    )
```

```python
import functools
import jax
import jax.numpy as jnp
from jax import lax
from jax.experimental import pallas as pl
from jax.experimental.pallas import tpu as pltpu
from jax.sharding import PartitionSpec as P

D = 4096
SPAN = 64
NBR = 2
RLEN = 128
CH_SEQ = 8
NB_SEQ = 16
ENC_CAP = 24


epsilon = 1e-05


def partner_2(block, axis, stride):
    count = lax.axis_size(axis)
    route = []
    for low in range(count):
        high = low | 1 << stride
        if high != low and high < count:
            route += [(low, high), (high, low)]
    return lax.ppermute(block, axis, route)


def passed_along(block, axis, distance):
    devices = range(lax.axis_size(axis))
    route = [(i - distance, i) for i in devices if i - distance in devices]
    return lax.ppermute(block, axis, route)


def project_fold(weight, piece):
    width = piece.shape[-1]
    flat_rows = piece.reshape(-1, width)
    mine = lax.all_to_all(weight, ("mp", "enc"), split_axis=0, concat_axis=1, tiled=True)
    partial = jnp.dot(flat_rows, mine, preferred_element_type=jnp.float32)
    running = lax.psum_scatter(partial, ("mp", "enc"), scatter_dimension=1, tiled=True)
    widened = flat_rows.astype(jnp.float32)
    squares = lax.psum(jnp.sum(widened * widened, axis=1), ("mp", "enc"))
    return (running, squares)


def normalized(carry, factor):
    running, squares = carry
    scale_rows = lax.rsqrt(squares / D + epsilon) * factor
    return (running * scale_rows[:, None]).astype(jnp.bfloat16)


def routing_plan(slot_target, counts, pair_cap):
    seq_count = counts.shape[0]
    seq_here = lax.axis_index("seq")
    live_count = jnp.sum(jnp.where(jnp.arange(seq_count) == seq_here, counts, 0))
    slot_ids = jnp.arange(ENC_CAP)
    live_slots = slot_ids < live_count
    owner_of = slot_target // NB_SEQ
    position = slot_target % NB_SEQ
    same_owner = (
        (owner_of[:, None] == owner_of[None, :])
        & live_slots[None, :]
        & (slot_ids[None, :] < slot_ids[:, None])
    )
    rank_within = jnp.sum(same_owner.astype(jnp.int32), axis=1)
    target_slot = owner_of * pair_cap + rank_within
    buffer_ids = jnp.arange(seq_count * pair_cap)
    chosen = (buffer_ids[:, None] == target_slot[None, :]) & live_slots[None, :]
    sent_ids = jnp.sum(jnp.where(chosen, position[None, :] + 1, 0), axis=1) - 1
    return (chosen, sent_ids.reshape(seq_count, pair_cap))


def pack_rows(chosen, payload, seq_count, pair_cap):
    packed = jnp.dot(chosen.astype(jnp.bfloat16), payload, preferred_element_type=jnp.float32)
    return packed.astype(jnp.bfloat16).reshape(seq_count, pair_cap, payload.shape[1])


def place_rows(received, received_ids):
    flat_rows = received.reshape(-1, received.shape[-1])
    picker = received_ids.reshape(1, -1) == jnp.arange(NB_SEQ)[:, None]
    placed = jnp.dot(picker.astype(jnp.bfloat16), flat_rows, preferred_element_type=jnp.float32)
    return placed.astype(jnp.bfloat16)


def local(tokens, nbr_feats, counts, slot_target, w_query, w_keyval):
    seq_count = lax.axis_size("seq")
    pair_cap = max(2, 2 * NB_SEQ // seq_count)
    head_size = w_keyval.shape[1]
    chosen, sent_ids = routing_plan(slot_target, counts, pair_cap)
    folded = project_fold(w_keyval, nbr_feats)
    encoded = normalized(folded, 1.0).reshape(ENC_CAP, RLEN * head_size)
    packed = pack_rows(chosen, encoded, seq_count, pair_cap)
    received, received_ids = (
        lax.all_to_all(packed, "seq", split_axis=0, concat_axis=0, tiled=True),
        lax.all_to_all(sent_ids, "seq", split_axis=0, concat_axis=0, tiled=True),
    )
    own_half = place_rows(received, received_ids).reshape(NB_SEQ, RLEN, head_size)
    partner = partner_2(own_half, "enc", 0)
    first_lane = lax.axis_index("enc") == 0
    key_rows = jnp.where(first_lane, own_half, partner).reshape(CH_SEQ, NBR * RLEN, head_size)
    value_rows = jnp.where(first_lane, partner, own_half).reshape(CH_SEQ, NBR * RLEN, head_size)
    prior_keys, prior_values = passed_along((key_rows[-1], value_rows[-1]), "seq", 1)
    context_keys = jnp.concatenate([prior_keys[None], key_rows[:-1]], axis=0)
    context_values = jnp.concatenate([prior_values[None], value_rows[:-1]], axis=0)
    folded_tokens = project_fold(w_query, tokens)
    queries = normalized(folded_tokens, head_size ** (-0.5)).reshape(CH_SEQ, SPAN, head_size)
    scores = jnp.einsum("cqd,ckd->cqk", queries, context_keys, preferred_element_type=jnp.float32)
    weights = jax.nn.softmax(scores, axis=-1).astype(jnp.bfloat16)
    attended = jnp.einsum(
        "cqk,ckd->cqd", weights, context_values, preferred_element_type=jnp.float32
    )
    return attended.astype(jnp.bfloat16).reshape(CH_SEQ * SPAN, head_size)


CHUNKS = 4
CROWS = RLEN // 2 // CHUNKS
CFLAT = ENC_CAP * CROWS


def fused(
    S, cap, trow, cnt, feats, tokens, wq, wkv, out,
    xb, tb, wown, woth, sown, ssend, srecv, town, tsend, trecv, ss, ssr,
    enc, zs, zr, zl, ctx, qb, qs, tab, tabr, pidx_v, lidx_v, pidx, lidx,
    lsem, send, recv,
):
    f32 = jnp.float32
    g, r, m, e = (lax.axis_index(a) for a in ("groups", "seq", "mp", "enc"))
    pg, pm, pe = 1 - g, 1 - m, 1 - e
    K = feats.shape[2]
    half = tokens.shape[0] // 2
    C = CHUNKS
    partner, across, beside = {"enc": pe}, {"mp": pm}, {"groups": pg}

    ids = {}
    total = 0
    for name, count in (
        ("wx", 2), ("wo", 2), ("wf", 2), ("wy", 2), ("wg", 2), ("x", C), ("t", 1), ("ss", 1),
        ("s", C), ("ts", 1), ("tab", S), ("z", C * S), ("fwd", C), ("pr0", C), ("pr1", C), ("q", 1),
    ):
        ids[name] = total
        total += count

    def rc(src, dst, name, at, device):
        i = ids[name] + at
        return pltpu.make_async_remote_copy(
            src_ref=src, dst_ref=dst, send_sem=send.at[i], recv_sem=recv.at[i],
            device_id=device, device_id_type=pl.DeviceIdType.MESH,
        )

    def landed(dst, name, at, device):
        rc(dst, dst, name, at, device).wait_recv()

    def lanes(index):
        return pl.ds(pl.multiple_of(index * 128, 128), 128)

    def rows(start, size):
        return pl.ds(pl.multiple_of(start, 16), size)

    def zdev(d):
        return {"seq": lax.rem(r + d, S)}

    barrier = pltpu.get_barrier_semaphore()
    for d in range(S):
        for other in (False, True):
            if d or other:
                device = dict(zdev(d), enc=pe if other else e)
                pl.semaphore_signal(
                    barrier, inc=1, device_id=device, device_id_type=pl.DeviceIdType.MESH
                )
    for device in (across, beside):
        pl.semaphore_signal(barrier, inc=1, device_id=device, device_id_type=pl.DeviceIdType.MESH)
    pl.semaphore_wait(barrier, 2 * S + 1)

    weights = (wkv, wq)
    done = []

    def begin(copy):
        copy.start()
        done.append(copy)

    def piece(k, part, side):
        return woth.at[k, rows(part * K, K), lanes(side)]

    def weight_across(k):
        begin(rc(weights[k].at[rows(2 * K * pm + K * g, K), :], piece(k, g, e), "wx", k, across))

    def weight_local(k):
        source = weights[k].at[rows(2 * K * m, 2 * K), :]
        target = wown.at[k, :, lanes(e)]
        begin(rc(source, target, "wo", k, partner))
        return pltpu.make_async_copy(source, target, lsem.at[C + k])

    def own_chunk(c):
        return pltpu.make_async_copy(
            feats.at[:, rows(CROWS * C * e + CROWS * c, CROWS), :], xb.at[e, c], lsem.at[c]
        )

    def sent_chunk(c):
        return rc(
            feats.at[:, rows(CROWS * C * pe + CROWS * c, CROWS), :], xb.at[e, c], "x", c, partner
        )

    weight_across(0)
    local_kv = weight_local(0)
    local_kv.start()
    for c in range(C):
        sent_chunk(c).start()
        own_chunk(c).start()
    weight_across(1)
    local_q = weight_local(1)
    local_q.start()
    begin(rc(tokens.at[rows(half * pe, half), :], tb.at[e], "t", 0, partner))
    local_t = pltpu.make_async_copy(tokens.at[rows(half * e, half), :], tb.at[e], lsem.at[C + 2])
    local_t.start()

    t_row = trow[...]
    iota = lambda shape, axis: lax.broadcasted_iota(jnp.int32, shape, axis)
    E = ENC_CAP
    t_col = jnp.sum(jnp.where(iota((E, E), 0) == iota((E, E), 1), t_row, 0), axis=1, keepdims=True)
    live = jnp.sum(jnp.where(iota((1, S), 1) == r, cnt[...], 0), axis=1, keepdims=True)
    same = (
        ((t_col >> 4) == (t_row >> 4)) & (iota((E, E), 1) < live) & (iota((E, E), 1) < iota((E, E), 0))
    )
    rank = jnp.sum(jnp.where(same, 1, 0), axis=1, keepdims=True)
    at_lane = iota((E, 128), 1)
    slot = iota((E, 128), 0)
    is_live = slot < live
    wanted = ((t_col >> 4) * cap + rank == at_lane) & is_live
    source_row = jnp.sum(jnp.where(wanted, slot, 0), axis=0, keepdims=True)
    held = (t_col == at_lane) & is_live
    place_row = jnp.sum(jnp.where(held, r * cap + rank, 0), axis=0, keepdims=True)
    pidx_v[...] = jnp.broadcast_to(source_row, (8, 128))
    tab[...] = jnp.broadcast_to(place_row, (8, 128))
    pack_copy = pltpu.make_async_copy(pidx_v, pidx, lsem.at[C + 3])
    pack_copy.start()
    for d in range(1, S):
        begin(rc(tab, tabr.at[d], "tab", d, zdev(d)))
    tabr[0] = tab[...]

    ss[...] = jnp.zeros_like(ss)
    eye = iota((128, 128), 0) == iota((128, 128), 1)

    def as_rows(column):
        blocks = column.reshape(-1, 128, 1)
        return jnp.sum(jnp.where(eye[None], blocks, 0.0), axis=1)

    def as_column(lined):
        blocks = jnp.where(eye[None], lined[:, None, :], 0.0)
        return jnp.sum(blocks, axis=2, keepdims=True).reshape(-1, 1)

    def squares(block):
        wide = block.astype(f32)
        return jnp.sum(wide * wide, axis=1, keepdims=True)

    def product(first, second, weight, k):
        return jnp.dot(first, weight[k, :K, :], preferred_element_type=f32) + jnp.dot(
            second, weight[k, K:, :], preferred_element_type=f32
        )

    def chunk_rows(c):
        return xb[0, c].reshape(CFLAT, K), xb[1, c].reshape(CFLAT, K)

    def first_pass(c, carry):
        own_chunk(c).wait()
        landed(xb.at[pe, c], "x", c, partner)
        one, two = chunk_rows(c)
        ss[c, 0 : CFLAT // 128, :] = as_rows(squares(one) + squares(two))
        sown[c] = product(one, two, wown, 0)
        return carry

    def spread_across(k):
        landed(piece(k, g, e), "wx", k, across)
        begin(rc(piece(k, g, e), piece(k, g, e), "wy", k, beside))
        begin(rc(piece(k, g, e), piece(k, g, e), "wf", k, partner))

    def spread_beside(k):
        landed(piece(k, pg, e), "wy", k, beside)
        begin(rc(piece(k, pg, e), piece(k, pg, e), "wg", k, partner))

    def spread_end(k):
        landed(piece(k, g, pe), "wf", k, partner)
        landed(piece(k, pg, pe), "wg", k, partner)

    local_kv.wait()
    landed(wown.at[0, :, lanes(pe)], "wo", 0, partner)
    spread_across(0)
    lax.fori_loop(0, C // 2, first_pass, 0)
    spread_beside(0)
    spread_across(1)
    lax.fori_loop(C // 2, C, first_pass, 0)
    local_q.wait()
    landed(wown.at[1, :, lanes(pe)], "wo", 1, partner)
    local_t.wait()
    landed(tb.at[pe], "t", 0, partner)
    ss[C, 0 : half // 128, :] = as_rows(squares(tb[0]) + squares(tb[1]))
    begin(rc(ss, ssr, "ss", 0, across))
    spread_beside(1)
    spread_end(0)

    def partial_copy(c):
        return rc(ssend.at[c], srecv.at[c], "s", c, across)

    def second_pass(c, carry):
        one, two = chunk_rows(c)
        ssend[c] = product(one, two, woth, 0)
        partial_copy(c).start()
        return carry

    lax.fori_loop(0, C, second_pass, 0)
    spread_end(1)
    tsend[...] = product(tb[0], tb[1], woth, 1)
    begin(rc(tsend, trecv, "ts", 0, across))
    town[...] = product(tb[0], tb[1], wown, 1)

    for d in range(1, S):
        landed(tabr.at[d], "tab", d, zdev(d))
    places = tabr[0]
    for d in range(1, S):
        places = places + tabr[d]
    lidx_v[...] = places
    place_copy = pltpu.make_async_copy(lidx_v, lidx, lsem.at[C + 4])
    place_copy.start()
    pack_copy.wait()
    place_copy.wait()

    @pl.when(r == 0)
    def _():
        ctx[0:2] = jnp.zeros((2,) + ctx.shape[1:], ctx.dtype)

    def z_copy(c, d):
        return rc(zs.at[c, lax.rem(r + d, S)], zr.at[c, r], "z", c * S + d, zdev(d))

    def z_landed(c, d):
        source = lax.rem(r + S - d, S)
        landed(zr.at[c, source], "z", c * S + d, {"seq": source})

    def ctx_rows(side, c):
        return rows(CROWS * C * side + CROWS * c, CROWS)

    def own_rows(side, c):
        return ctx.at[pl.ds(2, NB_SEQ), ctx_rows(side, c), :]

    def forward_copy(c):
        return rc(own_rows(e, c), own_rows(e, c), "fwd", c, partner)

    def prior_copy(c, same_core):
        return rc(
            ctx.at[pl.ds(NB_SEQ, 2), ctx_rows(e, c), :],
            ctx.at[pl.ds(0, 2), ctx_rows(e, c), :],
            "pr0" if same_core else "pr1", c,
            {"seq": lax.rem(r + 1, S), "enc": e if same_core else pe},
        )

    landed(ssr, "ss", 0, across)

    def factor(at, count):
        lined = ss[at, 0:count, :] + ssr[at, 0:count, :]
        return lax.rsqrt(as_column(lined) / D + epsilon)

    def encode(c):
        landed(srecv.at[c], "s", c, across)
        scaled = (sown[c] + srecv[c]) * factor(c, CFLAT // 128)
        enc[c] = scaled.astype(jnp.bfloat16).reshape(E, CROWS, 256)
        for d in list(range(1, S)) + [0]:
            dst = lax.rem(r + d, S)
            for k in range(cap):
                block = enc[c, pidx[0, dst * cap + k]]
                if d:
                    zs[c, dst, k] = block
                else:
                    zr[c, dst, k] = block
            if d:
                z_copy(c, d).start()

    def place(c):
        for d in range(1, S):
            z_landed(c, d)
        zl[...] = zr[c].reshape(zl.shape)
        for l in list(range(NB_SEQ - 1, -1, -1)):
            where = lidx[0, r * NB_SEQ + l]
            ctx[2 + l, ctx_rows(e, c), :] = zl[where]
        @pl.when(r < S - 1)
        def _():
            prior_copy(c, True).start()
            prior_copy(c, False).start()
        forward_copy(c).start()

    def third_pass(c, carry):
        encode(c)
        place(c - 1)
        return carry

    encode(0)
    lax.fori_loop(1, C, third_pass, 0)

    landed(trecv, "ts", 0, across)
    scaled = (town[...] + trecv[...]) * (factor(C, half // 128) * 128 ** (-0.5))
    rounded = scaled.astype(jnp.bfloat16)
    first = e == 0
    qb[e] = jnp.where(first, rounded[:, :128], rounded[:, 128:])
    qs[...] = jnp.where(first, rounded[:, 128:], rounded[:, :128])
    begin(rc(qs, qb.at[e], "q", 0, partner))

    place(C - 1)
    landed(qb.at[pe], "q", 0, partner)

    def settle(c, carry):
        landed(own_rows(pe, c), "fwd", c, partner)

        @pl.when(r > 0)
        def _():
            back = lax.rem(r + S - 1, S)
            landed(ctx.at[pl.ds(0, 2), ctx_rows(e, c), :], "pr0", c, {"seq": back})
            landed(ctx.at[pl.ds(0, 2), ctx_rows(pe, c), :], "pr1", c, {"seq": back, "enc": pe})

        return carry

    lax.fori_loop(0, C, settle, 0)

    spans = half // SPAN

    def attend(c, carry):
        queries = qb[c // spans, rows(c % spans * SPAN, SPAN), :]
        pair = ctx[pl.ds(2 * c, 2)].reshape(NBR * RLEN, 256)
        scores = lax.dot_general(
            queries, pair[:, :128], (((1,), (1,)), ((), ())), preferred_element_type=f32
        )
        raised = jnp.exp(scores - jnp.max(scores, axis=1, keepdims=True))
        weight = (raised / jnp.sum(raised, axis=1, keepdims=True)).astype(jnp.bfloat16)
        mixed = jnp.dot(weight, pair[:, 128:], preferred_element_type=f32)
        out[rows(c * SPAN, SPAN), :] = mixed.astype(jnp.bfloat16)
        return carry

    lax.fori_loop(0, 2 * spans, attend, 0)

    def drain(c, carry):
        sent_chunk(c).wait_send()
        partial_copy(c).wait_send()
        for d in range(1, S):
            z_copy(c, d).wait_send()
        forward_copy(c).wait_send()

        @pl.when(r < S - 1)
        def _():
            prior_copy(c, True).wait_send()
            prior_copy(c, False).wait_send()

        return carry

    lax.fori_loop(0, C, drain, 0)
    for copy in done:
        copy.wait_send()


def local_fused(tokens, nbr_feats, counts, slot_target, w_query, w_keyval):
    S = lax.axis_size("seq")
    cap = max(2, 2 * NB_SEQ // S)
    K = tokens.shape[1]
    half = tokens.shape[0] // 2
    C = CHUNKS
    bf, f32, i32 = jnp.bfloat16, jnp.float32, jnp.int32
    anywhere = pl.BlockSpec(memory_space=pl.ANY)
    vmem = pl.BlockSpec(memory_space=pltpu.VMEM)
    return pl.pallas_call(
        functools.partial(fused, S, cap),
        out_shape=jax.ShapeDtypeStruct((2 * half, 128), bf),
        in_specs=[vmem, vmem] + [anywhere] * 4,
        out_specs=vmem,
        scratch_shapes=[
            pltpu.VMEM((2, C, ENC_CAP, CROWS, K), bf),
            pltpu.VMEM((2, half, K), bf),
            pltpu.VMEM((2, 2 * K, 256), bf),
            pltpu.VMEM((2, 2 * K, 256), bf),
            pltpu.VMEM((C, CFLAT, 256), f32),
            pltpu.VMEM((C, CFLAT, 256), f32),
            pltpu.VMEM((C, CFLAT, 256), f32),
            pltpu.VMEM((half, 256), f32),
            pltpu.VMEM((half, 256), f32),
            pltpu.VMEM((half, 256), f32),
            pltpu.VMEM((C + 1, 8, 128), f32),
            pltpu.VMEM((C + 1, 8, 128), f32),
            pltpu.VMEM((C, ENC_CAP, CROWS, 256), bf),
            pltpu.VMEM((C, S, cap, CROWS, 256), bf),
            pltpu.VMEM((C, S, cap, CROWS, 256), bf),
            pltpu.VMEM((S * cap, CROWS, 256), bf),
            pltpu.VMEM((NB_SEQ + 2, RLEN, 256), bf),
            pltpu.VMEM((2, half, 128), bf),
            pltpu.VMEM((half, 128), bf),
            pltpu.VMEM((8, 128), i32),
            pltpu.VMEM((S, 8, 128), i32),
            pltpu.VMEM((8, 128), i32),
            pltpu.VMEM((8, 128), i32),
            pltpu.SMEM((8, 128), i32),
            pltpu.SMEM((8, 128), i32),
            pltpu.SemaphoreType.DMA((C + 5,)),
            pltpu.SemaphoreType.DMA((14 + 6 * C + S + C * S,)),
            pltpu.SemaphoreType.DMA((14 + 6 * C + S + C * S,)),
        ],
        compiler_params=pltpu.CompilerParams(
            collective_id=0, has_side_effects=True, vmem_limit_bytes=56 << 20
        ),
    )(slot_target.reshape(1, -1), counts.reshape(1, -1), nbr_feats, tokens, w_query, w_keyval)


def solution(mesh):
    small = mesh.shape["mp"] == 2 and mesh.shape["groups"] == 2 and mesh.shape["seq"] <= 8
    placed = (
        P(("groups", "seq"), ("mp", "enc")),
        P(("groups", "seq"), None, ("mp", "enc")),
        P("groups"),
        P(("groups", "seq")),
        P(None, ("mp", "enc")),
        P(None, ("mp", "enc")),
    )
    return jax.shard_map(
        local_fused if small else local,
        mesh=mesh,
        in_specs=placed,
        out_specs=P(("groups", "seq"), ("mp", "enc")),
        check_vma=False,
    )
```

```python
import functools
import jax
import jax.numpy as jnp
from jax import lax
from jax.experimental import pallas as pl
from jax.experimental.pallas import tpu as pltpu
from jax.sharding import PartitionSpec as P

D = 4096
SPAN = 64
NBR = 2
RLEN = 128
CH_SEQ = 8
NB_SEQ = 16
ENC_CAP = 24


epsilon = 1e-05


def partner_2(block, axis, stride):
    count = lax.axis_size(axis)
    route = []
    for low in range(count):
        high = low | 1 << stride
        if high != low and high < count:
            route += [(low, high), (high, low)]
    return lax.ppermute(block, axis, route)


def passed_along(block, axis, distance):
    devices = range(lax.axis_size(axis))
    route = [(i - distance, i) for i in devices if i - distance in devices]
    return lax.ppermute(block, axis, route)


def project_fold(weight, piece):
    width = piece.shape[-1]
    flat_rows = piece.reshape(-1, width)
    mine = lax.all_to_all(weight, ("mp", "enc"), split_axis=0, concat_axis=1, tiled=True)
    partial = jnp.dot(flat_rows, mine, preferred_element_type=jnp.float32)
    running = lax.psum_scatter(partial, ("mp", "enc"), scatter_dimension=1, tiled=True)
    widened = flat_rows.astype(jnp.float32)
    squares = lax.psum(jnp.sum(widened * widened, axis=1), ("mp", "enc"))
    return (running, squares)


def normalized(carry, factor):
    running, squares = carry
    scale_rows = lax.rsqrt(squares / D + epsilon) * factor
    return (running * scale_rows[:, None]).astype(jnp.bfloat16)


def routing_plan(slot_target, counts, pair_cap):
    seq_count = counts.shape[0]
    seq_here = lax.axis_index("seq")
    live_count = jnp.sum(jnp.where(jnp.arange(seq_count) == seq_here, counts, 0))
    slot_ids = jnp.arange(ENC_CAP)
    live_slots = slot_ids < live_count
    owner_of = slot_target // NB_SEQ
    position = slot_target % NB_SEQ
    same_owner = (
        (owner_of[:, None] == owner_of[None, :])
        & live_slots[None, :]
        & (slot_ids[None, :] < slot_ids[:, None])
    )
    rank_within = jnp.sum(same_owner.astype(jnp.int32), axis=1)
    target_slot = owner_of * pair_cap + rank_within
    buffer_ids = jnp.arange(seq_count * pair_cap)
    chosen = (buffer_ids[:, None] == target_slot[None, :]) & live_slots[None, :]
    sent_ids = jnp.sum(jnp.where(chosen, position[None, :] + 1, 0), axis=1) - 1
    return (chosen, sent_ids.reshape(seq_count, pair_cap))


def pack_rows(chosen, payload, seq_count, pair_cap):
    packed = jnp.dot(chosen.astype(jnp.bfloat16), payload, preferred_element_type=jnp.float32)
    return packed.astype(jnp.bfloat16).reshape(seq_count, pair_cap, payload.shape[1])


def place_rows(received, received_ids):
    flat_rows = received.reshape(-1, received.shape[-1])
    picker = received_ids.reshape(1, -1) == jnp.arange(NB_SEQ)[:, None]
    placed = jnp.dot(picker.astype(jnp.bfloat16), flat_rows, preferred_element_type=jnp.float32)
    return placed.astype(jnp.bfloat16)


def local(tokens, nbr_feats, counts, slot_target, w_query, w_keyval):
    seq_count = lax.axis_size("seq")
    pair_cap = max(2, 2 * NB_SEQ // seq_count)
    head_size = w_keyval.shape[1]
    chosen, sent_ids = routing_plan(slot_target, counts, pair_cap)
    folded = project_fold(w_keyval, nbr_feats)
    encoded = normalized(folded, 1.0).reshape(ENC_CAP, RLEN * head_size)
    packed = pack_rows(chosen, encoded, seq_count, pair_cap)
    received, received_ids = (
        lax.all_to_all(packed, "seq", split_axis=0, concat_axis=0, tiled=True),
        lax.all_to_all(sent_ids, "seq", split_axis=0, concat_axis=0, tiled=True),
    )
    own_half = place_rows(received, received_ids).reshape(NB_SEQ, RLEN, head_size)
    partner = partner_2(own_half, "enc", 0)
    first_lane = lax.axis_index("enc") == 0
    key_rows = jnp.where(first_lane, own_half, partner).reshape(CH_SEQ, NBR * RLEN, head_size)
    value_rows = jnp.where(first_lane, partner, own_half).reshape(CH_SEQ, NBR * RLEN, head_size)
    prior_keys, prior_values = passed_along((key_rows[-1], value_rows[-1]), "seq", 1)
    context_keys = jnp.concatenate([prior_keys[None], key_rows[:-1]], axis=0)
    context_values = jnp.concatenate([prior_values[None], value_rows[:-1]], axis=0)
    folded_tokens = project_fold(w_query, tokens)
    queries = normalized(folded_tokens, head_size ** (-0.5)).reshape(CH_SEQ, SPAN, head_size)
    scores = jnp.einsum("cqd,ckd->cqk", queries, context_keys, preferred_element_type=jnp.float32)
    weights = jax.nn.softmax(scores, axis=-1).astype(jnp.bfloat16)
    attended = jnp.einsum(
        "cqk,ckd->cqd", weights, context_values, preferred_element_type=jnp.float32
    )
    return attended.astype(jnp.bfloat16).reshape(CH_SEQ * SPAN, head_size)


CHUNKS = 4
CROWS = RLEN // 2 // CHUNKS
CFLAT = ENC_CAP * CROWS


def fused(
    S, cap, trow, cnt, feats, tokens, wq, wkv, out,
    xb, tb, wown, woth, sown, ssend, srecv, town, tsend, trecv, ss, ssr,
    enc, zs, zr, zl, ctx, qb, qs, tab, tabr, pidx_v, lidx_v, pidx, lidx,
    lsem, send, recv,
):
    f32 = jnp.float32
    g, r, m, e = (lax.axis_index(a) for a in ("groups", "seq", "mp", "enc"))
    pg, pm, pe = 1 - g, 1 - m, 1 - e
    K = feats.shape[2]
    half = tokens.shape[0] // 2
    C = CHUNKS
    partner, across, beside = {"enc": pe}, {"mp": pm}, {"groups": pg}

    ids = {}
    total = 0
    for name, count in (
        ("wx", 8), ("wo", 2), ("wf", 8), ("wy", 8), ("wg", 8), ("x", C), ("t", 1), ("ss", 1),
        ("s", C), ("ts", 1), ("tab", S), ("z", C * S), ("fwd", C), ("pr0", C), ("pr1", C), ("q", 1),
    ):
        ids[name] = total
        total += count

    def rc(src, dst, name, at, device):
        i = ids[name] + at
        return pltpu.make_async_remote_copy(
            src_ref=src, dst_ref=dst, send_sem=send.at[i], recv_sem=recv.at[i],
            device_id=device, device_id_type=pl.DeviceIdType.MESH,
        )

    def landed(dst, name, at, device):
        rc(dst, dst, name, at, device).wait_recv()

    def lanes(index):
        return pl.ds(pl.multiple_of(index * 128, 128), 128)

    def rows(start, size):
        return pl.ds(pl.multiple_of(start, 16), size)

    def zdev(d):
        return {"seq": lax.rem(r + d, S)}

    barrier = pltpu.get_barrier_semaphore()
    for d in range(S):
        for other in (False, True):
            if d or other:
                device = dict(zdev(d), enc=pe if other else e)
                pl.semaphore_signal(
                    barrier, inc=1, device_id=device, device_id_type=pl.DeviceIdType.MESH
                )
    for device in (across, beside):
        pl.semaphore_signal(barrier, inc=1, device_id=device, device_id_type=pl.DeviceIdType.MESH)
    pl.semaphore_wait(barrier, 2 * S + 1)

    weights = (wkv, wq)
    done = []

    def begin(copy):
        copy.start()
        done.append(copy)

    Q = K // 4

    def piece(k, part, i, side):
        return woth.at[k, rows(part * K + i * Q, Q), lanes(side)]

    def weight_across(k):
        for i in range(4):
            source = weights[k].at[rows(2 * K * pm + K * g + i * Q, Q), :]
            begin(rc(source, piece(k, g, i, e), "wx", 4 * k + i, across))

    def weight_local(k):
        source = weights[k].at[rows(2 * K * m, 2 * K), :]
        target = wown.at[k, :, lanes(e)]
        begin(rc(source, target, "wo", k, partner))
        return pltpu.make_async_copy(source, target, lsem.at[C + k])

    def own_chunk(c):
        return pltpu.make_async_copy(
            feats.at[:, rows(CROWS * C * e + CROWS * c, CROWS), :], xb.at[e, c], lsem.at[c]
        )

    def sent_chunk(c):
        return rc(
            feats.at[:, rows(CROWS * C * pe + CROWS * c, CROWS), :], xb.at[e, c], "x", c, partner
        )

    weight_across(0)
    local_kv = weight_local(0)
    local_kv.start()
    for c in range(C):
        sent_chunk(c).start()
        own_chunk(c).start()
    local_q = weight_local(1)
    local_q.start()
    begin(rc(tokens.at[rows(half * pe, half), :], tb.at[e], "t", 0, partner))
    local_t = pltpu.make_async_copy(tokens.at[rows(half * e, half), :], tb.at[e], lsem.at[C + 2])
    local_t.start()

    t_row = trow[...]
    iota = lambda shape, axis: lax.broadcasted_iota(jnp.int32, shape, axis)
    E = ENC_CAP
    t_col = jnp.sum(jnp.where(iota((E, E), 0) == iota((E, E), 1), t_row, 0), axis=1, keepdims=True)
    live = jnp.sum(jnp.where(iota((1, S), 1) == r, cnt[...], 0), axis=1, keepdims=True)
    same = (
        ((t_col >> 4) == (t_row >> 4)) & (iota((E, E), 1) < live) & (iota((E, E), 1) < iota((E, E), 0))
    )
    rank = jnp.sum(jnp.where(same, 1, 0), axis=1, keepdims=True)
    at_lane = iota((E, 128), 1)
    slot = iota((E, 128), 0)
    is_live = slot < live
    wanted = ((t_col >> 4) * cap + rank == at_lane) & is_live
    source_row = jnp.sum(jnp.where(wanted, slot, 0), axis=0, keepdims=True)
    held = (t_col == at_lane) & is_live
    place_row = jnp.sum(jnp.where(held, r * cap + rank, 0), axis=0, keepdims=True)
    pidx_v[...] = jnp.broadcast_to(source_row, (8, 128))
    tab[...] = jnp.broadcast_to(place_row, (8, 128))
    pack_copy = pltpu.make_async_copy(pidx_v, pidx, lsem.at[C + 3])
    pack_copy.start()
    for d in range(1, S):
        begin(rc(tab, tabr.at[d], "tab", d, zdev(d)))
    tabr[0] = tab[...]

    ss[...] = jnp.zeros_like(ss)
    eye = iota((128, 128), 0) == iota((128, 128), 1)

    def as_rows(column):
        blocks = column.reshape(-1, 128, 1)
        return jnp.sum(jnp.where(eye[None], blocks, 0.0), axis=1)

    def as_column(lined):
        blocks = jnp.where(eye[None], lined[:, None, :], 0.0)
        return jnp.sum(blocks, axis=2, keepdims=True).reshape(-1, 1)

    def squares(block):
        wide = block.astype(f32)
        return jnp.sum(wide * wide, axis=1, keepdims=True)

    def product(first, second, weight, k):
        return jnp.dot(first, weight[k, :K, :], preferred_element_type=f32) + jnp.dot(
            second, weight[k, K:, :], preferred_element_type=f32
        )

    def chunk_rows(c):
        return xb[0, c].reshape(CFLAT, K), xb[1, c].reshape(CFLAT, K)

    def first_pass(c, carry):
        own_chunk(c).wait()
        landed(xb.at[pe, c], "x", c, partner)
        one, two = chunk_rows(c)
        ss[c, 0 : CFLAT // 128, :] = as_rows(squares(one) + squares(two))
        sown[c] = product(one, two, wown, 0)
        return carry

    def spread_across(k, i):
        here = piece(k, g, i, e)
        landed(here, "wx", 4 * k + i, across)
        begin(rc(here, here, "wy", 4 * k + i, beside))
        begin(rc(here, here, "wf", 4 * k + i, partner))

    def spread_beside(k, i):
        here = piece(k, pg, i, e)
        landed(here, "wy", 4 * k + i, beside)
        begin(rc(here, here, "wg", 4 * k + i, partner))

    def spread_end(k):
        for i in range(4):
            landed(piece(k, g, i, pe), "wf", 4 * k + i, partner)
            landed(piece(k, pg, i, pe), "wg", 4 * k + i, partner)

    spread_across(0, 0)
    spread_across(0, 1)
    local_kv.wait()
    landed(wown.at[0, :, lanes(pe)], "wo", 0, partner)
    lax.fori_loop(0, 1, first_pass, 0)
    spread_across(0, 2)
    spread_across(0, 3)
    weight_across(1)
    spread_beside(0, 0)
    spread_beside(0, 1)
    lax.fori_loop(1, 2, first_pass, 0)
    spread_beside(0, 2)
    spread_beside(0, 3)
    lax.fori_loop(2, C, first_pass, 0)
    spread_end(0)

    def partial_copy(c):
        return rc(ssend.at[c], srecv.at[c], "s", c, across)

    def second_pass(c, carry):
        one, two = chunk_rows(c)
        ssend[c] = product(one, two, woth, 0)
        partial_copy(c).start()
        return carry

    lax.fori_loop(0, 2, second_pass, 0)
    local_t.wait()
    landed(tb.at[pe], "t", 0, partner)
    ss[C, 0 : half // 128, :] = as_rows(squares(tb[0]) + squares(tb[1]))
    begin(rc(ss, ssr, "ss", 0, across))
    for c in range(2, C):
        one, two = chunk_rows(c)
        ssend[c] = product(one, two, woth, 0)
    local_q.wait()
    landed(wown.at[1, :, lanes(pe)], "wo", 1, partner)
    town[...] = product(tb[0], tb[1], wown, 1)
    for i in range(4):
        spread_across(1, i)
    for i in range(4):
        spread_beside(1, i)
    spread_end(1)
    tsend[...] = product(tb[0], tb[1], woth, 1)

    for d in range(1, S):
        landed(tabr.at[d], "tab", d, zdev(d))
    places = tabr[0]
    for d in range(1, S):
        places = places + tabr[d]
    lidx_v[...] = places
    place_copy = pltpu.make_async_copy(lidx_v, lidx, lsem.at[C + 4])
    place_copy.start()
    pack_copy.wait()
    place_copy.wait()

    @pl.when(r == 0)
    def _():
        ctx[0:2] = jnp.zeros((2,) + ctx.shape[1:], ctx.dtype)

    def z_copy(c, d):
        return rc(zs.at[c, lax.rem(r + d, S)], zr.at[c, r], "z", c * S + d, zdev(d))

    def z_landed(c, d):
        source = lax.rem(r + S - d, S)
        landed(zr.at[c, source], "z", c * S + d, {"seq": source})

    def ctx_rows(side, c):
        return rows(CROWS * C * side + CROWS * c, CROWS)

    def own_rows(side, c):
        return ctx.at[pl.ds(2, NB_SEQ), ctx_rows(side, c), :]

    def forward_copy(c):
        return rc(own_rows(e, c), own_rows(e, c), "fwd", c, partner)

    def prior_copy(c, same_core):
        return rc(
            ctx.at[pl.ds(NB_SEQ, 2), ctx_rows(e, c), :],
            ctx.at[pl.ds(0, 2), ctx_rows(e, c), :],
            "pr0" if same_core else "pr1", c,
            {"seq": lax.rem(r + 1, S), "enc": e if same_core else pe},
        )

    landed(ssr, "ss", 0, across)

    def factor(at, count):
        lined = ss[at, 0:count, :] + ssr[at, 0:count, :]
        return lax.rsqrt(as_column(lined) / D + epsilon)

    def encode(c):
        landed(srecv.at[c], "s", c, across)

        @pl.when(c + 2 < C)
        def _():
            partial_copy(c + 2).start()

        @pl.when(c + 2 == C)
        def _():
            rc(tsend, trecv, "ts", 0, across).start()

        scaled = (sown[c] + srecv[c]) * factor(c, CFLAT // 128)
        enc[c] = scaled.astype(jnp.bfloat16).reshape(E, CROWS, 256)
        for d in list(range(1, S)) + [0]:
            dst = lax.rem(r + d, S)
            for k in range(cap):
                block = enc[c, pidx[0, dst * cap + k]]
                if d:
                    zs[c, dst, k] = block
                else:
                    zr[c, dst, k] = block
            if d:
                z_copy(c, d).start()

    def place(c):
        for d in range(1, S):
            z_landed(c, d)
        zl[...] = zr[c].reshape(zl.shape)
        for l in list(range(NB_SEQ - 1, -1, -1)):
            where = lidx[0, r * NB_SEQ + l]
            ctx[2 + l, ctx_rows(e, c), :] = zl[where]
        @pl.when(r < S - 1)
        def _():
            prior_copy(c, True).start()
            prior_copy(c, False).start()
        forward_copy(c).start()

    def third_pass(c, carry):
        encode(c)
        place(c - 1)
        return carry

    encode(0)
    lax.fori_loop(1, C, third_pass, 0)

    landed(trecv, "ts", 0, across)
    scaled = (town[...] + trecv[...]) * (factor(C, half // 128) * 128 ** (-0.5))
    rounded = scaled.astype(jnp.bfloat16)
    first = e == 0
    qb[e] = jnp.where(first, rounded[:, :128], rounded[:, 128:])
    qs[...] = jnp.where(first, rounded[:, 128:], rounded[:, :128])
    begin(rc(qs, qb.at[e], "q", 0, partner))

    place(C - 1)
    landed(qb.at[pe], "q", 0, partner)

    def settle(c, carry):
        landed(own_rows(pe, c), "fwd", c, partner)

        @pl.when(r > 0)
        def _():
            back = lax.rem(r + S - 1, S)
            landed(ctx.at[pl.ds(0, 2), ctx_rows(e, c), :], "pr0", c, {"seq": back})
            landed(ctx.at[pl.ds(0, 2), ctx_rows(pe, c), :], "pr1", c, {"seq": back, "enc": pe})

        return carry

    lax.fori_loop(0, C, settle, 0)

    spans = half // SPAN

    def attend(c):
        queries = qb[c // spans, rows(c % spans * SPAN, SPAN), :]
        pair = ctx[pl.ds(2 * c, 2)].reshape(NBR * RLEN, 256)
        scores = lax.dot_general(
            queries, pair[:, :128], (((1,), (1,)), ((), ())), preferred_element_type=f32
        )
        raised = jnp.exp(scores - jnp.max(scores, axis=1, keepdims=True))
        weight = (raised / jnp.sum(raised, axis=1, keepdims=True)).astype(jnp.bfloat16)
        mixed = jnp.dot(weight, pair[:, 128:], preferred_element_type=f32)
        out[rows(c * SPAN, SPAN), :] = mixed.astype(jnp.bfloat16)

    for c in range(2 * spans):
        attend(c)

    def drain(c, carry):
        sent_chunk(c).wait_send()
        partial_copy(c).wait_send()
        for d in range(1, S):
            z_copy(c, d).wait_send()
        forward_copy(c).wait_send()

        @pl.when(r < S - 1)
        def _():
            prior_copy(c, True).wait_send()
            prior_copy(c, False).wait_send()

        return carry

    lax.fori_loop(0, C, drain, 0)
    rc(tsend, trecv, "ts", 0, across).wait_send()
    for copy in done:
        copy.wait_send()


def local_fused(tokens, nbr_feats, counts, slot_target, w_query, w_keyval):
    S = lax.axis_size("seq")
    cap = max(2, 2 * NB_SEQ // S)
    K = tokens.shape[1]
    half = tokens.shape[0] // 2
    C = CHUNKS
    bf, f32, i32 = jnp.bfloat16, jnp.float32, jnp.int32
    anywhere = pl.BlockSpec(memory_space=pl.ANY)
    vmem = pl.BlockSpec(memory_space=pltpu.VMEM)
    return pl.pallas_call(
        functools.partial(fused, S, cap),
        out_shape=jax.ShapeDtypeStruct((2 * half, 128), bf),
        in_specs=[vmem, vmem] + [anywhere] * 4,
        out_specs=vmem,
        scratch_shapes=[
            pltpu.VMEM((2, C, ENC_CAP, CROWS, K), bf),
            pltpu.VMEM((2, half, K), bf),
            pltpu.VMEM((2, 2 * K, 256), bf),
            pltpu.VMEM((2, 2 * K, 256), bf),
            pltpu.VMEM((C, CFLAT, 256), f32),
            pltpu.VMEM((C, CFLAT, 256), f32),
            pltpu.VMEM((C, CFLAT, 256), f32),
            pltpu.VMEM((half, 256), f32),
            pltpu.VMEM((half, 256), f32),
            pltpu.VMEM((half, 256), f32),
            pltpu.VMEM((C + 1, 8, 128), f32),
            pltpu.VMEM((C + 1, 8, 128), f32),
            pltpu.VMEM((C, ENC_CAP, CROWS, 256), bf),
            pltpu.VMEM((C, S, cap, CROWS, 256), bf),
            pltpu.VMEM((C, S, cap, CROWS, 256), bf),
            pltpu.VMEM((S * cap, CROWS, 256), bf),
            pltpu.VMEM((NB_SEQ + 2, RLEN, 256), bf),
            pltpu.VMEM((2, half, 128), bf),
            pltpu.VMEM((half, 128), bf),
            pltpu.VMEM((8, 128), i32),
            pltpu.VMEM((S, 8, 128), i32),
            pltpu.VMEM((8, 128), i32),
            pltpu.VMEM((8, 128), i32),
            pltpu.SMEM((8, 128), i32),
            pltpu.SMEM((8, 128), i32),
            pltpu.SemaphoreType.DMA((C + 5,)),
            pltpu.SemaphoreType.DMA((38 + 6 * C + S + C * S,)),
            pltpu.SemaphoreType.DMA((38 + 6 * C + S + C * S,)),
        ],
        compiler_params=pltpu.CompilerParams(
            collective_id=0, has_side_effects=True, vmem_limit_bytes=56 << 20
        ),
    )(slot_target.reshape(1, -1), counts.reshape(1, -1), nbr_feats, tokens, w_query, w_keyval)


def solution(mesh):
    small = mesh.shape["mp"] == 2 and mesh.shape["groups"] == 2 and mesh.shape["seq"] <= 8
    placed = (
        P(("groups", "seq"), ("mp", "enc")),
        P(("groups", "seq"), None, ("mp", "enc")),
        P("groups"),
        P(("groups", "seq")),
        P(None, ("mp", "enc")),
        P(None, ("mp", "enc")),
    )
    return jax.shard_map(
        local_fused if small else local,
        mesh=mesh,
        in_specs=placed,
        out_specs=P(("groups", "seq"), ("mp", "enc")),
        check_vma=False,
    )
```
